32 devices in a mesh: segment: 2 (over core), expert: 16 (over z, y, x).
Axes of the slice: x: 2, y: 2, z: 4, core: 2. Of those that a mesh axis runs over, the one named last changes fastest.
Arguments:
- saved_input: bfloat16 [2, 2, 1024, 2048], P('segment', None, 'expert'), may hold values from -6 to 6
- out_grad: bfloat16 [2, 1024, 2048], P(None, 'expert'), may hold values from -6 to 6
- expert_ids: int32 [2, 2, 1024, 2], P('segment', None, 'expert'), may hold values from 0 to 15, all different within a row; in each aligned block of 64 rows (0 to 63, 64 to 127, ..., all dimensions but the last counted through in order) at most 16 rows name the same one
- router_weights: float32 [2, 2, 1024, 2], P('segment', None, 'expert'), may hold values from 0.1 to 0.9
- w_gate: bfloat16 [2, 16, 2048, 384], P('segment', 'expert'), may hold values from -0.125 to 0.125
- w_up: bfloat16 [2, 16, 2048, 384], P('segment', 'expert'), may hold values from -0.125 to 0.125
- w_down: bfloat16 [2, 16, 384, 2048], P('segment', 'expert'), may hold values from -0.3125 to 0.3125
- eigenbasis: bfloat16 [2, 16, 384, 384], P('segment', 'expert'), may hold values from -0.3125 to 0.3125
Outputs:
- input_grad: bfloat16 [2, 2, 1024, 2048], P('segment', None, 'expert')
- rotated_grad: bfloat16 [2, 16, 384, 2048], P('segment', 'expert')
- ekfac_scales: float32 [2, 16, 384, 2048], P('segment', 'expert')
The draws below stay inside these ranges and needn't reach their ends.
Inputs may be any that keep to these rules, and one draw needn't show every extreme that they name: `expert_ids`: the two experts of a token differ. In each layer and micro-batch, at most 16 rows of one block of 64 tokens choose the same expert, and some block reaches 16.
All inputs are finite; a program needn't handle non-finite values.
Results may differ from the reference program's by a relative error of at most 0.0085.
Values may be sent and summed in bfloat16 or wider, within the bound.
A program may use at most 128 MiB of HBM per device.

```python
import math
import jax
import jax.numpy as jnp
import numpy as np
from jax import lax

D = 2048
FF = 384
M = 2
TOK_TICK = 64
EXPERTS = 16
LAYERS = 2
TOKENS = 1024
CAP = 16
N_EXPERT = 16


def level_of(rng, extent, cuts, smallest, top_value):
    factor_of = 1.0
    for axis_at, parts in cuts:
        steps = jax.random.uniform(jax.random.fold_in(jax.random.fold_in(rng, 6), axis_at), (parts,), jnp.float32, smallest / len(cuts), top_value / len(cuts))
        factor_of = factor_of * jnp.repeat(jnp.exp(steps), extent[axis_at] // parts).reshape((-1,) + (1,) * (len(extent) - 1 - axis_at))
    return factor_of


def routed_block(own_key, own, number, rows, count, top, limit, lean):
    order = jax.random.permutation(own_key, count)
    packed, usual = portions_of(count, rows * top, limit, lean, True), portions_of(count, rows * top, limit, lean, False)
    places = jnp.arange(count)

    def named(tallies, turn):
        used = int((tallies > 0).sum())
        fixed = max(1, used // 4)
        moved = fixed + (places - fixed + turn * (used - fixed)) % max(1, count - fixed)
        return jnp.zeros((count,), jnp.int32).at[order[jnp.where(places < fixed, places, moved)]].set(jnp.asarray(tallies, jnp.int32))

    tallies = jnp.where(number % 4 == 0, named(packed, number // 4), named(usual, number - number // 4 - 1))
    mixed = jax.random.permutation(jax.random.fold_in(own, 3), count)
    giver, receiver = mixed[0:count // 2 * 2:2], mixed[1:count // 2 * 2:2]
    margin = jnp.minimum(tallies[giver] - 1, limit - tallies[receiver]) // 2
    margin = jnp.where((giver == order[0]) | (receiver == order[0]) | (tallies[receiver] == 0), 0, jnp.maximum(margin, 0))
    moved = jax.random.randint(jax.random.fold_in(own, 4), (count // 2,), 0, 1 << 20) % (margin + 1)
    tallies = tallies.at[giver].add(-moved).at[receiver].add(moved)
    labels = jnp.searchsorted(jnp.cumsum(tallies), jnp.arange(rows * top), side="right").astype(jnp.int32)
    table = labels.reshape(top, rows).T
    table = table[jax.random.permutation(jax.random.fold_in(own, 1), rows)]
    turn = jax.random.randint(jax.random.fold_in(own, 2), (rows, 1), 0, top)
    return jnp.take_along_axis(table, (jnp.arange(top)[None, :] + turn) % top, axis=1)


def portions_of(count, total, bound, lean, full):
    portions = [(1 << 20) // math.isqrt(standing ** lean) + 1 for standing in range(1, count + 1)]
    largest = bound if full else min(bound, max(-(-total // count), total * portions[0] // sum(portions)))
    least = 1 if total - largest >= count - 1 else 0
    holding, spare = [largest] + [least] * (count - 1), total - largest - least * (count - 1)
    while spare > 0:
        candidates = [i for i in range(1, count) if holding[i] < largest] or [i for i in range(1, count) if holding[i] < bound]
        whole, remaining = sum([portions[i] for i in candidates]), spare
        for i in candidates:
            extra = min(bound - holding[i], max(1, remaining * portions[i] // whole), spare)
            holding[i] = holding[i] + extra
            spare = spare - extra
    return np.array(holding)


def scatter_about(key, shape, width, bound, shards=(), kind=jnp.bfloat16):
    values = jax.random.normal(key, shape, jnp.float32) * width
    if len(shards) > 0:
        values = level_of(key, shape, shards, -0.22, 0.18) * values
    return jnp.clip(values, min=-bound, max=bound).astype(kind)


def setup_inputs(seed: int = 0) -> dict:
    key_of = jax.random.split(jax.random.key(seed), 9)
    saved_input = scatter_about(key_of[0], (LAYERS, M, TOKENS, D), 1.0, 6.0, ((0, 2), (2, 16)))
    out_grad = scatter_about(key_of[1], (M, TOKENS, D), 1.0, 6.0, ((1, 16),))
    expert_ids_keys = jax.random.split(jax.random.fold_in(key_of[2], 1), LAYERS * M * TOKENS // TOK_TICK)
    expert_ids_turns = jax.random.permutation(jax.random.fold_in(key_of[2], 3), LAYERS * M * TOKENS // TOK_TICK)
    expert_ids = jax.vmap(lambda own, number: routed_block(jax.random.fold_in(key_of[2], 2), own, number, TOK_TICK, EXPERTS, 2, CAP, 2))(expert_ids_keys, expert_ids_turns).reshape((LAYERS, M, TOKENS, 2))
    router_weights = jnp.clip(0.1 + 0.79999997 * jax.random.uniform(key_of[3], (LAYERS, M, TOKENS, 2), jnp.float32) ** level_of(key_of[3], (LAYERS, M, TOKENS, 2), ((0, 2), (2, 16)), -0.2, 0.2), 0.1, 0.9)
    w_gate = scatter_about(key_of[4], (LAYERS, EXPERTS, D, FF), D ** -0.5, 0.125, ((0, 2), (1, 16)))
    w_up = scatter_about(key_of[5], (LAYERS, EXPERTS, D, FF), D ** -0.5, 0.125, ((0, 2), (1, 16)))
    w_down = scatter_about(key_of[6], (LAYERS, EXPERTS, FF, D), FF ** -0.5, 0.3125, ((0, 2), (1, 16)))
    eigenbasis = scatter_about(key_of[7], (LAYERS, EXPERTS, FF, FF), FF ** -0.5, 0.3125, ((0, 2), (1, 16)))
    return {"saved_input": saved_input, "out_grad": out_grad, "expert_ids": expert_ids, "router_weights": router_weights, "w_gate": w_gate, "w_up": w_up, "w_down": w_down, "eigenbasis": eigenbasis}


def silu_parts(hidden_gate):
    sigma = jax.nn.sigmoid(hidden_gate)
    return hidden_gate * sigma, sigma * (1.0 + hidden_gate * (1.0 - sigma))


def expert_backward(inputs):
    x_rows, dy_rows, gate_mat, up_mat, down_mat, basis = inputs
    hidden_gate = jnp.dot(x_rows, gate_mat, preferred_element_type=jnp.float32)
    hidden_up = jnp.dot(x_rows, up_mat, preferred_element_type=jnp.float32)
    act, dact = silu_parts(hidden_gate)
    activ = (act * hidden_up).astype(jnp.bfloat16)
    grad_act = lax.dot_general(dy_rows, down_mat, (((1,), (1,)), ((), ())), preferred_element_type=jnp.float32)
    grad_gate = (grad_act * hidden_up * dact).astype(jnp.bfloat16)
    grad_up = (grad_act * act).astype(jnp.bfloat16)
    dx_rows = (lax.dot_general(grad_gate, gate_mat, (((1,), (1,)), ((), ())), preferred_element_type=jnp.float32)
               + lax.dot_general(grad_up, up_mat, (((1,), (1,)), ((), ())), preferred_element_type=jnp.float32)).astype(jnp.bfloat16)
    rotated = jnp.dot(activ, basis, preferred_element_type=jnp.float32).astype(jnp.bfloat16)
    grad_term = lax.dot_general(rotated, dy_rows, (((0,), (0,)), ((), ())), preferred_element_type=jnp.float32)
    rot_sq = (rotated.astype(jnp.float32) ** 2).astype(jnp.bfloat16)
    dy_sq = (dy_rows.astype(jnp.float32) ** 2).astype(jnp.bfloat16)
    scale_term = lax.dot_general(rot_sq, dy_sq, (((0,), (0,)), ((), ())), preferred_element_type=jnp.float32)
    return dx_rows, grad_term, scale_term


def slot_of(ids):
    flat = ids.reshape(N_EXPERT, TOK_TICK * 2)
    onehot = (flat[:, :, None] == jnp.arange(EXPERTS, dtype=jnp.int32)[None, None, :]).astype(jnp.int32)
    prior = jnp.cumsum(onehot, axis=1) - onehot
    rank = jnp.sum(prior * onehot, axis=2)
    source = jnp.arange(N_EXPERT, dtype=jnp.int32)[:, None]
    return (source * CAP + rank).reshape(-1).astype(jnp.int32)


def reference(saved_input, out_grad, expert_ids, router_weights, w_gate, w_up, w_down, eigenbasis):
    buffer_rows = N_EXPERT * CAP
    grads_in = [None] * LAYERS
    grad_sums = [None] * LAYERS
    scale_sums = [None] * LAYERS
    incoming = out_grad
    for layer in reversed(range(LAYERS)):
        grad_acc = jnp.zeros((EXPERTS, FF, D), jnp.float32)
        scale_acc = jnp.zeros((EXPERTS, FF, D), jnp.float32)
        layer_out = []
        for micro in range(M):
            tokens_in = saved_input[layer, micro]
            upstream = incoming[micro]
            ids = expert_ids[layer, micro]
            slots = slot_of(ids)
            flat_ids = ids.reshape(-1).astype(jnp.int32)
            x_rep = jnp.repeat(tokens_in, 2, axis=0)
            dy_rep = (router_weights[layer, micro].reshape(-1, 1) * jnp.repeat(upstream.astype(jnp.float32), 2, axis=0)).astype(jnp.bfloat16)
            x_buf = jnp.zeros((EXPERTS, buffer_rows, D), jnp.bfloat16).at[flat_ids, slots].set(x_rep)
            dy_buf = jnp.zeros((EXPERTS, buffer_rows, D), jnp.bfloat16).at[flat_ids, slots].set(dy_rep)
            dx_buf, grad_term, scale_term = lax.map(expert_backward, (x_buf, dy_buf, w_gate[layer], w_up[layer], w_down[layer], eigenbasis[layer]))
            grad_acc = grad_acc + grad_term
            scale_acc = scale_acc + scale_term
            back = dx_buf[flat_ids, slots].astype(jnp.float32).reshape(TOKENS, 2, D)
            layer_out.append((upstream.astype(jnp.float32) + back[:, 0] + back[:, 1]).astype(jnp.bfloat16))
        grads_in[layer] = jnp.stack(layer_out)
        incoming = grads_in[layer]
        grad_sums[layer] = (grad_acc * (1.0 / M)).astype(jnp.bfloat16)
        scale_sums[layer] = scale_acc * (1.0 / M)
    return (jnp.stack(grads_in), jnp.stack(grad_sums), jnp.stack(scale_sums))
```

```python
import functools

import jax
import jax.numpy as jnp
from jax import lax
from jax.experimental import pallas as pl
from jax.experimental.pallas import tpu as pltpu
from jax.sharding import PartitionSpec as P


def passed_along(block, axis, distance):
    devices = range(lax.axis_size(axis))
    route = [(i - distance, i) for i in devices if i - distance in devices]
    return lax.ppermute(block, axis, route)


def silu_parts(hidden_gate):
    sigma = jax.nn.sigmoid(hidden_gate)
    return (hidden_gate * sigma, sigma * (1.0 + hidden_gate * (1.0 - sigma)))


def project_forward(x_rows, gate_mat, up_mat):
    hidden_gate = jnp.dot(x_rows, gate_mat, preferred_element_type=jnp.float32)
    hidden_up = jnp.dot(x_rows, up_mat, preferred_element_type=jnp.float32)
    return (hidden_gate, hidden_up)


def expert_backward(hidden_gate, hidden_up, dy_rows, gate_mat, up_mat, down_mat, basis):
    act, dact = silu_parts(hidden_gate)
    activ = (act * hidden_up).astype(jnp.bfloat16)
    grad_act = lax.dot_general(
        dy_rows, down_mat, (((1,), (1,)), ((), ())), preferred_element_type=jnp.float32
    )
    grad_gate = (grad_act * hidden_up * dact).astype(jnp.bfloat16)
    grad_up = (grad_act * act).astype(jnp.bfloat16)
    dx_rows = (
        lax.dot_general(
            grad_gate, gate_mat, (((1,), (1,)), ((), ())), preferred_element_type=jnp.float32
        )
        + lax.dot_general(
            grad_up, up_mat, (((1,), (1,)), ((), ())), preferred_element_type=jnp.float32
        )
    ).astype(jnp.bfloat16)
    rotated = jnp.dot(activ, basis, preferred_element_type=jnp.float32).astype(jnp.bfloat16)
    rot_sq = (rotated.astype(jnp.float32) ** 2).astype(jnp.bfloat16)
    dy_sq = (dy_rows.astype(jnp.float32) ** 2).astype(jnp.bfloat16)
    return (dx_rows, rotated, rot_sq, dy_sq)


def dispatch_matrix(ids, expert_count, capacity):
    flat = ids.reshape(-1)
    pairs = flat.shape[0]
    onehot = (flat[:, None] == jnp.arange(expert_count, dtype=jnp.int32)[None, :]).astype(
        jnp.float32
    )
    row_pos = lax.broadcasted_iota(jnp.int32, (pairs, pairs), 0)
    col_pos = lax.broadcasted_iota(jnp.int32, (pairs, pairs), 1)
    earlier = (row_pos > col_pos).astype(jnp.float32)
    prior = jnp.dot(
        earlier, onehot, precision=lax.Precision.HIGHEST, preferred_element_type=jnp.float32
    )
    rank = jnp.sum(prior * onehot, axis=1).astype(jnp.int32)
    slots = flat * capacity + rank
    targets = jnp.arange(expert_count * capacity, dtype=jnp.int32)
    return (targets[:, None] == slots[None, :]).astype(jnp.bfloat16)


def spread_rows(matrix, token_rows):
    return jnp.dot(matrix, token_rows, preferred_element_type=jnp.float32).astype(jnp.bfloat16)


def shards(saved_input, out_grad, expert_ids, router_weights, w_gate, w_up, w_down, eigenbasis):
    segment_count = lax.axis_size("segment")
    expert_count = lax.axis_size("expert")
    segment_here = lax.axis_index("segment")
    micro_count = saved_input.shape[1]
    tokens_dev = saved_input.shape[2]
    width = saved_input.shape[3]
    capacity = max(2, 4 * tokens_dev // expert_count)
    buffer_rows = expert_count * capacity
    gate_mat = w_gate[0, 0]
    up_mat = w_up[0, 0]
    down_mat = w_down[0, 0]
    basis = eigenbasis[0, 0]
    hidden_width = gate_mat.shape[1]
    matrices = jnp.stack(
        [
            dispatch_matrix(expert_ids[0, micro], expert_count, capacity)
            for micro in range(micro_count)
        ]
    )
    x_send = jnp.stack(
        [
            spread_rows(matrices[micro], jnp.repeat(saved_input[0, micro], 2, axis=0))
            for micro in range(micro_count)
        ]
    )
    x_recv = lax.all_to_all(
        x_send.reshape(micro_count, expert_count, capacity, width),
        "expert",
        split_axis=1,
        concat_axis=1,
        tiled=True,
    )
    gate_all, up_all = project_forward(
        x_recv.reshape(micro_count * buffer_rows, width), gate_mat, up_mat
    )
    gate_all = gate_all.reshape(micro_count, buffer_rows, hidden_width)
    up_all = up_all.reshape(micro_count, buffer_rows, hidden_width)
    rotated_list = []
    dy_list = []
    rot_sq_list = []
    dy_sq_list = []
    grads_out = jnp.zeros((micro_count, tokens_dev, width), jnp.bfloat16)
    received = jnp.zeros((tokens_dev, width), jnp.bfloat16)
    zero_rows = jnp.zeros((tokens_dev, width), jnp.bfloat16)
    total_ticks = micro_count + segment_count - 1
    for tick_index in range(total_ticks):
        micro_now = tick_index - (segment_count - 1 - segment_here)
        valid = jnp.logical_and(micro_now >= 0, micro_now < micro_count)
        index = jnp.clip(micro_now, 0, micro_count - 1)
        last_grad = lax.dynamic_index_in_dim(out_grad, index, 0, keepdims=False)
        upstream = jnp.where(segment_here == segment_count - 1, last_grad, received)
        upstream = jnp.where(valid, upstream, zero_rows)
        matrix = lax.dynamic_index_in_dim(matrices, index, 0, keepdims=False)
        weights_now = lax.dynamic_index_in_dim(router_weights[0], index, 0, keepdims=False)
        dy_tok = (
            weights_now.reshape(-1, 1) * jnp.repeat(upstream.astype(jnp.float32), 2, axis=0)
        ).astype(jnp.bfloat16)
        dy_send = spread_rows(matrix, dy_tok).reshape(expert_count, capacity, width)
        dy_rows = lax.all_to_all(
            dy_send, "expert", split_axis=0, concat_axis=0, tiled=True
        ).reshape(buffer_rows, width)
        hidden_gate = lax.dynamic_index_in_dim(gate_all, index, 0, keepdims=False)
        hidden_up = lax.dynamic_index_in_dim(up_all, index, 0, keepdims=False)
        dx_rows, rotated, rot_sq, dy_sq = expert_backward(
            hidden_gate, hidden_up, dy_rows, gate_mat, up_mat, down_mat, basis
        )
        rotated_list.append(rotated)
        dy_list.append(dy_rows)
        rot_sq_list.append(rot_sq)
        dy_sq_list.append(dy_sq)
        back = lax.all_to_all(
            dx_rows.reshape(expert_count, capacity, width),
            "expert",
            split_axis=0,
            concat_axis=0,
            tiled=True,
        ).reshape(buffer_rows, width)
        picked = lax.dot_general(
            matrix, back, (((0,), (0,)), ((), ())), preferred_element_type=jnp.float32
        ).reshape(tokens_dev, 2, width)
        grad_in = (upstream.astype(jnp.float32) + picked[:, 0] + picked[:, 1]).astype(jnp.bfloat16)
        updated = lax.dynamic_update_index_in_dim(grads_out, grad_in, index, 0)
        grads_out = jnp.where(valid, updated, grads_out)
        if tick_index + 1 < total_ticks:
            received = passed_along(grad_in, "segment", -1)
    all_rotated = jnp.concatenate(rotated_list, axis=0)
    all_dy = jnp.concatenate(dy_list, axis=0)
    all_rot_sq = jnp.concatenate(rot_sq_list, axis=0)
    all_dy_sq = jnp.concatenate(dy_sq_list, axis=0)
    grad_sum = lax.dot_general(
        all_rotated, all_dy, (((0,), (0,)), ((), ())), preferred_element_type=jnp.float32
    )
    scale_sum = lax.dot_general(
        all_rot_sq, all_dy_sq, (((0,), (0,)), ((), ())), preferred_element_type=jnp.float32
    )
    rotated_grad = (grad_sum * (1.0 / micro_count)).astype(jnp.bfloat16)
    ekfac_scales = scale_sum * (1.0 / micro_count)
    return (grads_out[None], rotated_grad[None, None], ekfac_scales[None, None])


def dot_f32(a, b, dims):
    return lax.dot_general(a, b, (dims, ((), ())), preferred_element_type=jnp.float32)


def relay_kernel(
    cap,
    x_ref,
    og_ref,
    ids_ref,
    rw_ref,
    gate_hbm,
    up_hbm,
    down_hbm,
    basis_hbm,
    gin_out,
    rot_out,
    scale_out,
    gate,
    up,
    down,
    basis,
    x_send,
    x_recv,
    dy_send,
    dy_recv,
    dx_send,
    dx_recv,
    g_recv,
    gin,
    hid_g,
    hid_u,
    rot_t,
    rsq_t,
    spread_x,
    spread_dy,
    combine,
    rot_v,
    scale_v,
    w_sem,
    send_sem,
    recv_sem,
    self_sem,
    relay_send,
    relay_recv,
    out_sem,
):
    bf16 = jnp.bfloat16
    f32 = jnp.float32
    n = lax.axis_size("expert")
    segs = lax.axis_size("segment")
    me = lax.axis_index("expert")
    seg = lax.axis_index("segment")
    micros, tokens, width = x_ref.shape
    rows = n * cap
    is_last = seg == segs - 1
    is_first = seg == 0
    X, DY, DX = 0, 1, 2

    weights = [
        pltpu.make_async_copy(src, dst, w_sem.at[i])
        for i, (src, dst) in enumerate(
            ((gate_hbm, gate), (up_hbm, up), (down_hbm, down), (basis_hbm, basis))
        )
    ]
    for w in weights:
        w.start()

    barrier = pltpu.get_barrier_semaphore()

    def greet(d, carry):
        pl.semaphore_signal(barrier, inc=1, device_id={"expert": lax.rem(me + d, n)})
        return carry

    lax.fori_loop(1, n, greet, 0)

    @pl.when(seg > 0)
    def _():
        pl.semaphore_signal(barrier, inc=1, device_id={"segment": seg - 1})

    @pl.when(seg < segs - 1)
    def _():
        pl.semaphore_signal(barrier, inc=1, device_id={"segment": seg + 1})

    row_t = lax.broadcasted_iota(jnp.int32, (tokens, tokens), 0)
    col_t = lax.broadcasted_iota(jnp.int32, (tokens, tokens), 1)
    earlier = (row_t > col_t).astype(bf16)
    lanes = lax.broadcasted_iota(jnp.int32, (tokens, n), 1)
    slots_iota = lax.broadcasted_iota(jnp.int32, (tokens, rows), 1)
    for m in range(micros):
        ids0 = ids_ref[m, :, 0:1]
        ids1 = ids_ref[m, :, 1:2]
        hot0 = (lanes == ids0).astype(f32)
        hot1 = (lanes == ids1).astype(f32)
        prior = dot_f32(earlier, (hot0 + hot1).astype(bf16), ((1,), (0,)))
        rank0 = jnp.sum(prior * hot0, axis=1, keepdims=True).astype(jnp.int32)
        rank1 = jnp.sum(prior * hot1, axis=1, keepdims=True).astype(jnp.int32)
        pick0 = (slots_iota == ids0 * cap + rank0).astype(f32)
        pick1 = (slots_iota == ids1 * cap + rank1).astype(f32)
        both = pick0 + pick1
        combine[m] = both.astype(bf16)
        spread_x[m] = jnp.transpose(both).astype(bf16)
        spread_dy[m] = jnp.transpose(jnp.concatenate([pick0, pick1], axis=0)).astype(bf16)

    def spread(m, matrix, values, dst):
        step = min(512, width)
        for c in range(width // step):
            cols = slice(c * step, (c + 1) * step)
            dst[m, :, cols] = dot_f32(matrix, values(cols), ((1,), (0,))).astype(bf16)

    def block(i):
        return pl.ds(pl.multiple_of(i * cap, cap), cap)

    def push(kind, m, src, dst):
        pltpu.make_async_copy(
            src.at[m, block(me)], dst.at[m, block(me)], self_sem.at[kind, m]
        ).start()

        def one(d, carry):
            peer = lax.rem(me + d, n)
            pltpu.make_async_remote_copy(
                src_ref=src.at[m, block(peer)],
                dst_ref=dst.at[m, block(me)],
                send_sem=send_sem.at[kind, m],
                recv_sem=recv_sem.at[kind, m],
                device_id={"expert": peer},
            ).start()
            return carry

        lax.fori_loop(1, n, one, 0)

    def whole(kind, m, src, dst):
        part = pl.ds(0, (n - 1) * cap)
        return pltpu.make_async_remote_copy(
            src_ref=src.at[m, part],
            dst_ref=dst.at[m, part],
            send_sem=send_sem.at[kind, m],
            recv_sem=recv_sem.at[kind, m],
            device_id={"expert": lax.rem(me + 1, n)},
        )

    def arrive(kind, m, src, dst):
        pltpu.make_async_copy(
            src.at[m, block(me)], dst.at[m, block(me)], self_sem.at[kind, m]
        ).wait()
        whole(kind, m, src, dst).wait_recv()

    def send_x(m):
        spread(m, spread_x[m], lambda cols: x_ref[m, :, cols], x_send)
        push(X, m, x_send, x_recv)

    def send_dy(m, g_ref):
        w0 = rw_ref[m, :, 0:1]
        w1 = rw_ref[m, :, 1:2]

        def values(cols):
            g = g_ref[m, :, cols].astype(f32)
            return jnp.concatenate([(w0 * g).astype(bf16), (w1 * g).astype(bf16)], axis=0)

        spread(m, spread_dy[m], values, dy_send)
        push(DY, m, dy_send, dy_recv)

    def forward(m):
        arrive(X, m, x_send, x_recv)
        x = x_recv[m]
        hid_g[m] = dot_f32(x, gate[...], ((1,), (0,)))
        hid_u[m] = dot_f32(x, up[...], ((1,), (0,)))

    def backward(m):
        arrive(DY, m, dy_send, dy_recv)
        grad_act = dot_f32(dy_recv[m], down[...], ((1,), (1,)))
        hg = hid_g[m]
        hu = hid_u[m]
        act, dact = silu_parts(hg)
        grad_gate = (grad_act * hu * dact).astype(bf16)
        grad_up = (grad_act * act).astype(bf16)
        step = min(512, width)
        for c in range(width // step):
            cols = slice(c * step, (c + 1) * step)
            dx_send[m, :, cols] = (
                dot_f32(grad_gate, gate[cols, :], ((1,), (1,)))
                + dot_f32(grad_up, up[cols, :], ((1,), (1,)))
            ).astype(bf16)
        push(DX, m, dx_send, dx_recv)

    def rotate(m):
        act, _ = silu_parts(hid_g[m])
        activ = (act * hid_u[m]).astype(bf16)
        rotated = dot_f32(activ, basis[...], ((1,), (0,))).astype(bf16).astype(f32)
        turned = jnp.transpose(rotated)
        rot_t[m] = turned.astype(bf16)
        rsq_t[m] = (turned * turned).astype(bf16)

    def relay(m):
        return pltpu.make_async_remote_copy(
            src_ref=gin.at[m],
            dst_ref=g_recv.at[m],
            send_sem=relay_send.at[m],
            recv_sem=relay_recv.at[m],
            device_id={"segment": lax.rem(seg + segs - 1, segs)},
        )

    def gather_back(m, g_ref):
        arrive(DX, m, dx_send, dx_recv)
        step = min(512, width)
        for c in range(width // step):
            cols = slice(c * step, (c + 1) * step)
            picked = dot_f32(combine[m], dx_recv[m, :, cols], ((1,), (0,)))
            gin[m, :, cols] = (g_ref[m, :, cols].astype(f32) + picked).astype(bf16)

        @pl.when(seg > 0)
        def _():
            relay(m).start()

        pltpu.make_async_copy(gin.at[m], gin_out.at[m], out_sem.at[2 + m]).start()

    def statistics():
        step = min(256, width)

        def one(c, carry):
            cols = pl.ds(pl.multiple_of(c * step, step), step)
            grad = jnp.zeros((rot_v.shape[0], step), f32)
            scale = jnp.zeros((rot_v.shape[0], step), f32)
            for m in range(micros):
                dy = dy_recv[m, :, cols]
                wide = dy.astype(f32)
                grad = grad + dot_f32(rot_t[m], dy, ((1,), (0,)))
                scale = scale + dot_f32(rsq_t[m], (wide * wide).astype(bf16), ((1,), (0,)))
            rot_v[:, cols] = (grad * (1.0 / micros)).astype(bf16)
            scale_v[:, cols] = scale * (1.0 / micros)
            return carry

        lax.fori_loop(0, width // step, one, 0)
        pltpu.make_async_copy(rot_v, rot_out, out_sem.at[0]).start()
        pltpu.make_async_copy(scale_v, scale_out, out_sem.at[1]).start()

    def per_micro(fn):
        def one(m, carry):
            fn(m)
            return carry

        lax.fori_loop(0, micros, one, 0)

    neighbours = jnp.minimum(seg, 1) + jnp.minimum(segs - 1 - seg, 1)
    pl.semaphore_wait(barrier, n - 1 + neighbours)

    @pl.when(is_last)
    def _():
        def first(m):
            send_dy(m, og_ref)
            send_x(m)

        per_micro(first)
        for w in weights:
            w.wait()

        def second(m):
            forward(m)
            backward(m)

        per_micro(second)
        per_micro(rotate)
        per_micro(lambda m: gather_back(m, og_ref))
        statistics()

    @pl.when(jnp.logical_not(is_last))
    def _():
        per_micro(send_x)
        for w in weights:
            w.wait()
        per_micro(forward)
        per_micro(rotate)

        def third(m):
            relay(m).wait_recv()
            send_dy(m, g_recv)

        per_micro(third)
        per_micro(backward)
        statistics()
        per_micro(lambda m: gather_back(m, g_recv))

    def drain(m):
        whole(X, m, x_send, x_recv).wait_send()
        whole(DY, m, dy_send, dy_recv).wait_send()
        whole(DX, m, dx_send, dx_recv).wait_send()

        @pl.when(seg > 0)
        def _():
            relay(m).wait_send()

        pltpu.make_async_copy(gin.at[m], gin_out.at[m], out_sem.at[2 + m]).wait()

    per_micro(drain)
    pltpu.make_async_copy(rot_v, rot_out, out_sem.at[0]).wait()
    pltpu.make_async_copy(scale_v, scale_out, out_sem.at[1]).wait()


def fused_shards(
    saved_input, out_grad, expert_ids, router_weights, w_gate, w_up, w_down, eigenbasis
):
    n = lax.axis_size("expert")
    micros, tokens, width = saved_input.shape[1:]
    cap = max(2, 4 * tokens // n)
    if cap % 16:
        return shards(
            saved_input, out_grad, expert_ids, router_weights, w_gate, w_up, w_down, eigenbasis
        )
    rows = n * cap
    hidden = w_gate.shape[3]
    bf16 = jnp.bfloat16
    f32 = jnp.float32
    vmem = pl.BlockSpec(memory_space=pltpu.VMEM)
    anywhere = pl.BlockSpec(memory_space=pl.ANY)
    routed = pltpu.VMEM((micros, rows, width), bf16)
    grad_in, rotated_grad, scales = pl.pallas_call(
        functools.partial(relay_kernel, cap),
        name="relay",
        out_shape=(
            jax.ShapeDtypeStruct((micros, tokens, width), bf16),
            jax.ShapeDtypeStruct((hidden, width), bf16),
            jax.ShapeDtypeStruct((hidden, width), f32),
        ),
        in_specs=[vmem] * 4 + [anywhere] * 4,
        out_specs=(anywhere, anywhere, anywhere),
        scratch_shapes=[
            pltpu.VMEM((width, hidden), bf16),
            pltpu.VMEM((width, hidden), bf16),
            pltpu.VMEM((hidden, width), bf16),
            pltpu.VMEM((hidden, hidden), bf16),
            routed,
            routed,
            routed,
            routed,
            routed,
            routed,
            pltpu.VMEM((micros, tokens, width), bf16),
            pltpu.VMEM((micros, tokens, width), bf16),
            pltpu.VMEM((micros, rows, hidden), f32),
            pltpu.VMEM((micros, rows, hidden), f32),
            pltpu.VMEM((micros, hidden, rows), bf16),
            pltpu.VMEM((micros, hidden, rows), bf16),
            pltpu.VMEM((micros, rows, tokens), bf16),
            pltpu.VMEM((micros, rows, 2 * tokens), bf16),
            pltpu.VMEM((micros, tokens, rows), bf16),
            pltpu.VMEM((hidden, width), bf16),
            pltpu.VMEM((hidden, width), f32),
            pltpu.SemaphoreType.DMA((4,)),
            pltpu.SemaphoreType.DMA((3, micros)),
            pltpu.SemaphoreType.DMA((3, micros)),
            pltpu.SemaphoreType.DMA((3, micros)),
            pltpu.SemaphoreType.DMA((micros,)),
            pltpu.SemaphoreType.DMA((micros,)),
            pltpu.SemaphoreType.DMA((2 + micros,)),
        ],
        compiler_params=pltpu.CompilerParams(
            collective_id=0, has_side_effects=True, vmem_limit_bytes=62 << 20
        ),
    )(
        saved_input[0],
        out_grad,
        expert_ids[0],
        router_weights[0],
        w_gate[0, 0],
        w_up[0, 0],
        w_down[0, 0],
        eigenbasis[0, 0],
    )
    return (grad_in[None], rotated_grad[None, None], scales[None, None])


def solution(mesh):
    in_specs = (
        P("segment", None, "expert", None),
        P(None, "expert", None),
        P("segment", None, "expert", None),
        P("segment", None, "expert", None),
        P("segment", "expert", None, None),
        P("segment", "expert", None, None),
        P("segment", "expert", None, None),
        P("segment", "expert", None, None),
    )
    out_specs = (
        P("segment", None, "expert", None),
        P("segment", "expert", None, None),
        P("segment", "expert", None, None),
    )
    return jax.shard_map(
        fused_shards, mesh=mesh, in_specs=in_specs, out_specs=out_specs, check_vma=False)
```

```python
import functools

import jax
import jax.numpy as jnp
from jax import lax
from jax.experimental import pallas as pl
from jax.experimental.pallas import tpu as pltpu
from jax.sharding import PartitionSpec as P


def passed_along(block, axis, distance):
    devices = range(lax.axis_size(axis))
    route = [(i - distance, i) for i in devices if i - distance in devices]
    return lax.ppermute(block, axis, route)


def silu_parts(hidden_gate):
    sigma = jax.nn.sigmoid(hidden_gate)
    return (hidden_gate * sigma, sigma * (1.0 + hidden_gate * (1.0 - sigma)))


def project_forward(x_rows, gate_mat, up_mat):
    hidden_gate = jnp.dot(x_rows, gate_mat, preferred_element_type=jnp.float32)
    hidden_up = jnp.dot(x_rows, up_mat, preferred_element_type=jnp.float32)
    return (hidden_gate, hidden_up)


def expert_backward(hidden_gate, hidden_up, dy_rows, gate_mat, up_mat, down_mat, basis):
    act, dact = silu_parts(hidden_gate)
    activ = (act * hidden_up).astype(jnp.bfloat16)
    grad_act = lax.dot_general(
        dy_rows, down_mat, (((1,), (1,)), ((), ())), preferred_element_type=jnp.float32
    )
    grad_gate = (grad_act * hidden_up * dact).astype(jnp.bfloat16)
    grad_up = (grad_act * act).astype(jnp.bfloat16)
    dx_rows = (
        lax.dot_general(
            grad_gate, gate_mat, (((1,), (1,)), ((), ())), preferred_element_type=jnp.float32
        )
        + lax.dot_general(
            grad_up, up_mat, (((1,), (1,)), ((), ())), preferred_element_type=jnp.float32
        )
    ).astype(jnp.bfloat16)
    rotated = jnp.dot(activ, basis, preferred_element_type=jnp.float32).astype(jnp.bfloat16)
    rot_sq = (rotated.astype(jnp.float32) ** 2).astype(jnp.bfloat16)
    dy_sq = (dy_rows.astype(jnp.float32) ** 2).astype(jnp.bfloat16)
    return (dx_rows, rotated, rot_sq, dy_sq)


def dispatch_matrix(ids, expert_count, capacity):
    flat = ids.reshape(-1)
    pairs = flat.shape[0]
    onehot = (flat[:, None] == jnp.arange(expert_count, dtype=jnp.int32)[None, :]).astype(
        jnp.float32
    )
    row_pos = lax.broadcasted_iota(jnp.int32, (pairs, pairs), 0)
    col_pos = lax.broadcasted_iota(jnp.int32, (pairs, pairs), 1)
    earlier = (row_pos > col_pos).astype(jnp.float32)
    prior = jnp.dot(
        earlier, onehot, precision=lax.Precision.HIGHEST, preferred_element_type=jnp.float32
    )
    rank = jnp.sum(prior * onehot, axis=1).astype(jnp.int32)
    slots = flat * capacity + rank
    targets = jnp.arange(expert_count * capacity, dtype=jnp.int32)
    return (targets[:, None] == slots[None, :]).astype(jnp.bfloat16)


def spread_rows(matrix, token_rows):
    return jnp.dot(matrix, token_rows, preferred_element_type=jnp.float32).astype(jnp.bfloat16)


def shards(saved_input, out_grad, expert_ids, router_weights, w_gate, w_up, w_down, eigenbasis):
    segment_count = lax.axis_size("segment")
    expert_count = lax.axis_size("expert")
    segment_here = lax.axis_index("segment")
    micro_count = saved_input.shape[1]
    tokens_dev = saved_input.shape[2]
    width = saved_input.shape[3]
    capacity = max(2, 4 * tokens_dev // expert_count)
    buffer_rows = expert_count * capacity
    gate_mat = w_gate[0, 0]
    up_mat = w_up[0, 0]
    down_mat = w_down[0, 0]
    basis = eigenbasis[0, 0]
    hidden_width = gate_mat.shape[1]
    matrices = jnp.stack(
        [
            dispatch_matrix(expert_ids[0, micro], expert_count, capacity)
            for micro in range(micro_count)
        ]
    )
    x_send = jnp.stack(
        [
            spread_rows(matrices[micro], jnp.repeat(saved_input[0, micro], 2, axis=0))
            for micro in range(micro_count)
        ]
    )
    x_recv = lax.all_to_all(
        x_send.reshape(micro_count, expert_count, capacity, width),
        "expert",
        split_axis=1,
        concat_axis=1,
        tiled=True,
    )
    gate_all, up_all = project_forward(
        x_recv.reshape(micro_count * buffer_rows, width), gate_mat, up_mat
    )
    gate_all = gate_all.reshape(micro_count, buffer_rows, hidden_width)
    up_all = up_all.reshape(micro_count, buffer_rows, hidden_width)
    rotated_list = []
    dy_list = []
    rot_sq_list = []
    dy_sq_list = []
    grads_out = jnp.zeros((micro_count, tokens_dev, width), jnp.bfloat16)
    received = jnp.zeros((tokens_dev, width), jnp.bfloat16)
    zero_rows = jnp.zeros((tokens_dev, width), jnp.bfloat16)
    total_ticks = micro_count + segment_count - 1
    for tick_index in range(total_ticks):
        micro_now = tick_index - (segment_count - 1 - segment_here)
        valid = jnp.logical_and(micro_now >= 0, micro_now < micro_count)
        index = jnp.clip(micro_now, 0, micro_count - 1)
        last_grad = lax.dynamic_index_in_dim(out_grad, index, 0, keepdims=False)
        upstream = jnp.where(segment_here == segment_count - 1, last_grad, received)
        upstream = jnp.where(valid, upstream, zero_rows)
        matrix = lax.dynamic_index_in_dim(matrices, index, 0, keepdims=False)
        weights_now = lax.dynamic_index_in_dim(router_weights[0], index, 0, keepdims=False)
        dy_tok = (
            weights_now.reshape(-1, 1) * jnp.repeat(upstream.astype(jnp.float32), 2, axis=0)
        ).astype(jnp.bfloat16)
        dy_send = spread_rows(matrix, dy_tok).reshape(expert_count, capacity, width)
        dy_rows = lax.all_to_all(
            dy_send, "expert", split_axis=0, concat_axis=0, tiled=True
        ).reshape(buffer_rows, width)
        hidden_gate = lax.dynamic_index_in_dim(gate_all, index, 0, keepdims=False)
        hidden_up = lax.dynamic_index_in_dim(up_all, index, 0, keepdims=False)
        dx_rows, rotated, rot_sq, dy_sq = expert_backward(
            hidden_gate, hidden_up, dy_rows, gate_mat, up_mat, down_mat, basis
        )
        rotated_list.append(rotated)
        dy_list.append(dy_rows)
        rot_sq_list.append(rot_sq)
        dy_sq_list.append(dy_sq)
        back = lax.all_to_all(
            dx_rows.reshape(expert_count, capacity, width),
            "expert",
            split_axis=0,
            concat_axis=0,
            tiled=True,
        ).reshape(buffer_rows, width)
        picked = lax.dot_general(
            matrix, back, (((0,), (0,)), ((), ())), preferred_element_type=jnp.float32
        ).reshape(tokens_dev, 2, width)
        grad_in = (upstream.astype(jnp.float32) + picked[:, 0] + picked[:, 1]).astype(jnp.bfloat16)
        updated = lax.dynamic_update_index_in_dim(grads_out, grad_in, index, 0)
        grads_out = jnp.where(valid, updated, grads_out)
        if tick_index + 1 < total_ticks:
            received = passed_along(grad_in, "segment", -1)
    all_rotated = jnp.concatenate(rotated_list, axis=0)
    all_dy = jnp.concatenate(dy_list, axis=0)
    all_rot_sq = jnp.concatenate(rot_sq_list, axis=0)
    all_dy_sq = jnp.concatenate(dy_sq_list, axis=0)
    grad_sum = lax.dot_general(
        all_rotated, all_dy, (((0,), (0,)), ((), ())), preferred_element_type=jnp.float32
    )
    scale_sum = lax.dot_general(
        all_rot_sq, all_dy_sq, (((0,), (0,)), ((), ())), preferred_element_type=jnp.float32
    )
    rotated_grad = (grad_sum * (1.0 / micro_count)).astype(jnp.bfloat16)
    ekfac_scales = scale_sum * (1.0 / micro_count)
    return (grads_out[None], rotated_grad[None, None], ekfac_scales[None, None])


def dot_f32(a, b, dims):
    return lax.dot_general(a, b, (dims, ((), ())), preferred_element_type=jnp.float32)


def relay_kernel(
    cap,
    x_ref,
    og_ref,
    ids_ref,
    rw_ref,
    gate_hbm,
    up_hbm,
    down_hbm,
    basis_hbm,
    gin_out,
    rot_out,
    scale_out,
    gate,
    up,
    down,
    basis,
    x_send,
    x_recv,
    dy_send,
    dy_recv,
    dx_send,
    dx_recv,
    x_peer,
    g_peer,
    part_send,
    part_recv,
    own_part,
    g_recv,
    gin,
    hid_g,
    hid_u,
    rot_t,
    rsq_t,
    spread_m,
    combine,
    slot_w,
    ids_peer,
    rw_peer,
    rot_v,
    scale_v,
    w_sem,
    send_sem,
    recv_sem,
    self_sem,
    swap_send,
    swap_recv,
    meta_send,
    meta_recv,
    relay_send,
    relay_recv,
    out_sem,
):
    bf16 = jnp.bfloat16
    f32 = jnp.float32
    n = lax.axis_size("expert")
    segs = lax.axis_size("segment")
    me = lax.axis_index("expert")
    seg = lax.axis_index("segment")
    micros, tokens, width = x_ref.shape
    half = n // 2
    local = lax.rem(me, half)
    base = me - local
    partner = lax.rem(me + half, n)
    rows = half * cap
    OWN, PEER = 0, 1
    step = min(512, width)
    pieces = [slice(c * step, (c + 1) * step) for c in range(width // step)]
    is_last = seg == segs - 1
    inner = (me >= half) == (local < half // 2)
    X, DY, DX = 0, 1, 2
    GX, GG, GP = 0, 1, 2

    weights = [
        pltpu.make_async_copy(src, dst, w_sem.at[i])
        for i, (src, dst) in enumerate(
            ((gate_hbm, gate), (up_hbm, up), (down_hbm, down), (basis_hbm, basis))
        )
    ]
    for w in weights:
        w.start()

    barrier = pltpu.get_barrier_semaphore()

    def greet(d, carry):
        peer = base + lax.rem(local + d, half)
        pl.semaphore_signal(barrier, inc=1, device_id={"expert": peer})
        return carry

    lax.fori_loop(1, half, greet, 0)
    pl.semaphore_signal(barrier, inc=1, device_id={"expert": partner})

    @pl.when(seg > 0)
    def _():
        pl.semaphore_signal(barrier, inc=1, device_id={"segment": seg - 1})

    @pl.when(seg < segs - 1)
    def _():
        pl.semaphore_signal(barrier, inc=1, device_id={"segment": seg + 1})

    def block(side, i):
        return pl.ds(pl.multiple_of(side * rows + i * cap, cap), cap)

    def push(kind, side, m, src, dst):
        here = block(side, local)
        pltpu.make_async_copy(
            src.at[m, here], dst.at[m, here], self_sem.at[kind, side, m]
        ).start()

        def one(d, carry):
            other = lax.rem(local + d, half)
            pltpu.make_async_remote_copy(
                src_ref=src.at[m, block(side, other)],
                dst_ref=dst.at[m, here],
                send_sem=send_sem.at[kind, side, m],
                recv_sem=recv_sem.at[kind, side, m],
                device_id={"expert": base + other},
            ).start()
            return carry

        lax.fori_loop(1, half, one, 0)

    def whole(kind, side, m, src, dst):
        part = pl.ds(side * rows, (half - 1) * cap)
        return pltpu.make_async_remote_copy(
            src_ref=src.at[m, part],
            dst_ref=dst.at[m, part],
            send_sem=send_sem.at[kind, side, m],
            recv_sem=recv_sem.at[kind, side, m],
            device_id={"expert": base + lax.rem(local + 1, half)},
        )

    def arrive(kind, side, m, src, dst):
        here = block(side, local)
        pltpu.make_async_copy(
            src.at[m, here], dst.at[m, here], self_sem.at[kind, side, m]
        ).wait()
        whole(kind, side, m, src, dst).wait_recv()

    def swap(kind, m, src, dst):
        return pltpu.make_async_remote_copy(
            src_ref=src.at[m],
            dst_ref=dst.at[m],
            send_sem=swap_send.at[kind, m],
            recv_sem=swap_recv.at[kind, m],
            device_id={"expert": partner},
        )

    metas = [
        pltpu.make_async_remote_copy(
            src_ref=src,
            dst_ref=dst,
            send_sem=meta_send.at[i],
            recv_sem=meta_recv.at[i],
            device_id={"expert": partner},
        )
        for i, (src, dst) in enumerate(((ids_ref, ids_peer), (rw_ref, rw_peer)))
    ]

    def matrices(side, ids, rw):
        row_t = lax.broadcasted_iota(jnp.int32, (tokens, tokens), 0)
        col_t = lax.broadcasted_iota(jnp.int32, (tokens, tokens), 1)
        earlier = (row_t < col_t).astype(bf16)
        experts = lax.broadcasted_iota(jnp.int32, (n, tokens), 0)
        slots = lax.broadcasted_iota(jnp.int32, (rows, tokens), 0)
        for m in range(micros):
            ids0 = ids[m, 0:1, :]
            ids1 = ids[m, 1:2, :]
            hot0 = (experts == ids0).astype(f32)
            hot1 = (experts == ids1).astype(f32)
            prior = dot_f32((hot0 + hot1).astype(bf16), earlier, ((1,), (0,)))
            rank0 = jnp.sum(prior * hot0, axis=0, keepdims=True).astype(jnp.int32)
            rank1 = jnp.sum(prior * hot1, axis=0, keepdims=True).astype(jnp.int32)
            pick0 = (slots == (ids0 - base) * cap + rank0).astype(f32)
            pick1 = (slots == (ids1 - base) * cap + rank1).astype(f32)
            both = pick0 + pick1
            weighted = pick0 * rw[m, 0:1, :] + pick1 * rw[m, 1:2, :]
            spread_m[m, side] = both.astype(bf16)
            combine[m, side] = jnp.transpose(both).astype(bf16)
            slot_w[m, side] = jnp.sum(weighted, axis=1, keepdims=True)

    def send_x(side, m, src):
        for cols in pieces:
            moved = dot_f32(spread_m[m, side], src[m, :, cols], ((1,), (0,)))
            x_send[m, side * rows : (side + 1) * rows, cols] = moved.astype(bf16)
        push(X, side, m, x_send, x_recv)

    def send_dy(side, m, src):
        for cols in pieces:
            moved = dot_f32(spread_m[m, side], src[m, :, cols], ((1,), (0,)))
            dy_send[m, side * rows : (side + 1) * rows, cols] = (
                slot_w[m, side] * moved
            ).astype(bf16)
        push(DY, side, m, dy_send, dy_recv)

    def begin_x(m):
        pl.when(inner)(swap(GX, m, x_ref, x_peer).start)
        send_x(OWN, m, x_ref)
        pl.when(jnp.logical_not(inner))(swap(GX, m, x_ref, x_peer).start)

    def begin_dy(m, g_ref):
        pl.when(inner)(swap(GG, m, g_ref, g_peer).start)
        send_dy(OWN, m, g_ref)
        pl.when(jnp.logical_not(inner))(swap(GG, m, g_ref, g_peer).start)

    def peer_x(m):
        swap(GX, m, x_ref, x_peer).wait_recv()
        send_x(PEER, m, x_peer)

    def peer_dy(m, g_ref):
        swap(GG, m, g_ref, g_peer).wait_recv()
        send_dy(PEER, m, g_peer)

    def forward(m):
        arrive(X, OWN, m, x_send, x_recv)
        arrive(X, PEER, m, x_send, x_recv)
        x = x_recv[m]
        hid_g[m] = dot_f32(x, gate[...], ((1,), (0,)))
        hid_u[m] = dot_f32(x, up[...], ((1,), (0,)))

    def backward(m):
        arrive(DY, OWN, m, dy_send, dy_recv)
        arrive(DY, PEER, m, dy_send, dy_recv)
        grad_act = dot_f32(dy_recv[m], down[...], ((1,), (1,)))
        hg = hid_g[m]
        hu = hid_u[m]
        act, dact = silu_parts(hg)
        grad_gate = (grad_act * hu * dact).astype(bf16)
        grad_up = (grad_act * act).astype(bf16)
        for cols in pieces:
            dx_send[m, :, cols] = (
                dot_f32(grad_gate, gate[cols, :], ((1,), (1,)))
                + dot_f32(grad_up, up[cols, :], ((1,), (1,)))
            ).astype(bf16)
        push(DX, PEER, m, dx_send, dx_recv)
        push(DX, OWN, m, dx_send, dx_recv)

    def rotate(m):
        act, _ = silu_parts(hid_g[m])
        activ = (act * hid_u[m]).astype(bf16)
        rotated = dot_f32(activ, basis[...], ((1,), (0,))).astype(bf16).astype(f32)
        turned = jnp.transpose(rotated)
        rot_t[m] = turned.astype(bf16)
        rsq_t[m] = (turned * turned).astype(bf16)

    def relay(m):
        return pltpu.make_async_remote_copy(
            src_ref=gin.at[m],
            dst_ref=g_recv.at[m],
            send_sem=relay_send.at[m],
            recv_sem=relay_recv.at[m],
            device_id={"segment": lax.rem(seg + segs - 1, segs)},
        )

    def half_back(m):
        arrive(DX, PEER, m, dx_send, dx_recv)
        for cols in pieces:
            theirs = dot_f32(combine[m, PEER], dx_recv[m, rows:, cols], ((1,), (0,)))
            part_send[m, :, cols] = theirs.astype(bf16)
        swap(GP, m, part_send, part_recv).start()

    def own_back(m, g_ref):
        arrive(DX, OWN, m, dx_send, dx_recv)
        for cols in pieces:
            mine = dot_f32(combine[m, OWN], dx_recv[m, :rows, cols], ((1,), (0,)))
            own_part[m, :, cols] = g_ref[m, :, cols].astype(f32) + mine

    def finish(m):
        swap(GP, m, part_send, part_recv).wait_recv()
        gin[m] = (own_part[m] + part_recv[m].astype(f32)).astype(bf16)

        @pl.when(seg > 0)
        def _():
            relay(m).start()

        pltpu.make_async_copy(gin.at[m], gin_out.at[m], out_sem.at[2 + m]).start()

    def statistics():
        part = min(256, width)

        def one(c, carry):
            cols = pl.ds(pl.multiple_of(c * part, part), part)
            grad = jnp.zeros((rot_v.shape[0], part), f32)
            scale = jnp.zeros((rot_v.shape[0], part), f32)
            for m in range(micros):
                dy = dy_recv[m, :, cols]
                wide = dy.astype(f32)
                grad = grad + dot_f32(rot_t[m], dy, ((1,), (0,)))
                scale = scale + dot_f32(rsq_t[m], (wide * wide).astype(bf16), ((1,), (0,)))
            rot_v[:, cols] = (grad * (1.0 / micros)).astype(bf16)
            scale_v[:, cols] = scale * (1.0 / micros)
            return carry

        lax.fori_loop(0, width // part, one, 0)
        pltpu.make_async_copy(rot_v, rot_out, out_sem.at[0]).start()
        pltpu.make_async_copy(scale_v, scale_out, out_sem.at[1]).start()

    def per_micro(fn):
        def one(m, carry):
            fn(m)
            return carry

        lax.fori_loop(0, micros, one, 0)

    matrices(OWN, ids_ref, rw_ref)
    neighbours = jnp.minimum(seg, 1) + jnp.minimum(segs - 1 - seg, 1)
    pl.semaphore_wait(barrier, half + neighbours)
    for meta in metas:
        meta.start()

    @pl.when(is_last)
    def _():
        begin_dy(0, og_ref)
        begin_x(0)
        for meta in metas:
            meta.wait_recv()
        matrices(PEER, ids_peer, rw_peer)
        for w in weights:
            w.wait()

        def through(m, carry):
            peer_dy(m - 1, og_ref)
            begin_dy(m, og_ref)
            peer_x(m - 1)
            begin_x(m)
            forward(m - 1)
            backward(m - 1)
            return carry

        lax.fori_loop(1, micros, through, 0)
        peer_dy(micros - 1, og_ref)
        peer_x(micros - 1)
        forward(micros - 1)
        backward(micros - 1)

        def back(m):
            half_back(m)
            own_back(m, og_ref)
            finish(m)

        per_micro(back)
        per_micro(rotate)
        statistics()

    @pl.when(jnp.logical_not(is_last))
    def _():
        for meta in metas:
            meta.wait_recv()
        matrices(PEER, ids_peer, rw_peer)
        begin_x(0)
        peer_x(0)
        for w in weights:
            w.wait()
        forward(0)
        rotate(0)

        def begin(m):
            relay(m).wait_recv()
            begin_dy(m, g_recv)

        begin(0)

        def through(m, carry):
            begin_x(m)
            peer_dy(m - 1, g_recv)
            peer_x(m)
            begin(m)
            backward(m - 1)
            forward(m)
            rotate(m)
            return carry

        lax.fori_loop(1, micros, through, 0)
        peer_dy(micros - 1, g_recv)
        backward(micros - 1)
        half_back(0)
        statistics()
        own_back(0, g_recv)
        finish(0)

        def back(m, carry):
            half_back(m)
            own_back(m, g_recv)
            finish(m)
            return carry

        lax.fori_loop(1, micros, back, 0)

    for meta in metas:
        meta.wait_send()

    def drain(m):
        for side in (OWN, PEER):
            whole(X, side, m, x_send, x_recv).wait_send()
            whole(DY, side, m, dy_send, dy_recv).wait_send()
            whole(DX, side, m, dx_send, dx_recv).wait_send()
        swap(GX, m, x_ref, x_peer).wait_send()
        swap(GG, m, g_recv, g_peer).wait_send()
        swap(GP, m, part_send, part_recv).wait_send()

        @pl.when(seg > 0)
        def _():
            relay(m).wait_send()

        pltpu.make_async_copy(gin.at[m], gin_out.at[m], out_sem.at[2 + m]).wait()

    per_micro(drain)
    pltpu.make_async_copy(rot_v, rot_out, out_sem.at[0]).wait()
    pltpu.make_async_copy(scale_v, scale_out, out_sem.at[1]).wait()


def fused_shards(
    saved_input, out_grad, expert_ids, router_weights, w_gate, w_up, w_down, eigenbasis
):
    n = lax.axis_size("expert")
    micros, tokens, width = saved_input.shape[1:]
    cap = max(2, 4 * tokens // n)
    if cap % 16 or n % 2:
        return shards(
            saved_input, out_grad, expert_ids, router_weights, w_gate, w_up, w_down, eigenbasis
        )
    rows = n * cap
    hidden = w_gate.shape[3]
    bf16 = jnp.bfloat16
    f32 = jnp.float32
    vmem = pl.BlockSpec(memory_space=pltpu.VMEM)
    anywhere = pl.BlockSpec(memory_space=pl.ANY)
    in_hbm = pl.BlockSpec(memory_space=pltpu.MemorySpace.HBM)
    routed = pltpu.VMEM((micros, rows, width), bf16)
    block = pltpu.VMEM((micros, tokens, width), bf16)
    grad_in, rotated_grad, scales = pl.pallas_call(
        functools.partial(relay_kernel, cap),
        name="relay",
        out_shape=(
            jax.ShapeDtypeStruct((micros, tokens, width), bf16),
            jax.ShapeDtypeStruct((hidden, width), bf16),
            jax.ShapeDtypeStruct((hidden, width), f32),
        ),
        in_specs=[vmem] * 4 + [in_hbm] * 4,
        out_specs=(anywhere, anywhere, anywhere),
        scratch_shapes=[
            pltpu.VMEM((width, hidden), bf16),
            pltpu.VMEM((width, hidden), bf16),
            pltpu.VMEM((hidden, width), bf16),
            pltpu.VMEM((hidden, hidden), bf16),
            routed,
            routed,
            routed,
            routed,
            routed,
            routed,
            block,
            block,
            block,
            block,
            pltpu.VMEM((micros, tokens, width), f32),
            block,
            block,
            pltpu.VMEM((micros, rows, hidden), f32),
            pltpu.VMEM((micros, rows, hidden), f32),
            pltpu.VMEM((micros, hidden, rows), bf16),
            pltpu.VMEM((micros, hidden, rows), bf16),
            pltpu.VMEM((micros, 2, rows // 2, tokens), bf16),
            pltpu.VMEM((micros, 2, tokens, rows // 2), bf16),
            pltpu.VMEM((micros, 2, rows // 2, 1), f32),
            pltpu.VMEM((micros, 2, tokens), jnp.int32),
            pltpu.VMEM((micros, 2, tokens), f32),
            pltpu.VMEM((hidden, width), bf16),
            pltpu.VMEM((hidden, width), f32),
            pltpu.SemaphoreType.DMA((4,)),
            pltpu.SemaphoreType.DMA((3, 2, micros)),
            pltpu.SemaphoreType.DMA((3, 2, micros)),
            pltpu.SemaphoreType.DMA((3, 2, micros)),
            pltpu.SemaphoreType.DMA((3, micros)),
            pltpu.SemaphoreType.DMA((3, micros)),
            pltpu.SemaphoreType.DMA((2,)),
            pltpu.SemaphoreType.DMA((2,)),
            pltpu.SemaphoreType.DMA((micros,)),
            pltpu.SemaphoreType.DMA((micros,)),
            pltpu.SemaphoreType.DMA((2 + micros,)),
        ],
        compiler_params=pltpu.CompilerParams(
            collective_id=0, has_side_effects=True, vmem_limit_bytes=62 << 20
        ),
    )(
        saved_input[0],
        out_grad,
        jnp.swapaxes(expert_ids[0], 1, 2),
        jnp.swapaxes(router_weights[0], 1, 2),
        w_gate[0, 0],
        w_up[0, 0],
        w_down[0, 0],
        eigenbasis[0, 0],
    )
    return (grad_in[None], rotated_grad[None, None], scales[None, None])


def solution(mesh):
    in_specs = (
        P("segment", None, "expert", None),
        P(None, "expert", None),
        P("segment", None, "expert", None),
        P("segment", None, "expert", None),
        P("segment", "expert", None, None),
        P("segment", "expert", None, None),
        P("segment", "expert", None, None),
        P("segment", "expert", None, None),
    )
    out_specs = (
        P("segment", None, "expert", None),
        P("segment", "expert", None, None),
        P("segment", "expert", None, None),
    )
    return jax.shard_map(
        fused_shards, mesh=mesh, in_specs=in_specs, out_specs=out_specs, check_vma=False)
```

```python
import functools

import jax
import jax.numpy as jnp
from jax import lax
from jax.experimental import pallas as pl
from jax.experimental.pallas import tpu as pltpu
from jax.sharding import PartitionSpec as P


def passed_along(block, axis, distance):
    devices = range(lax.axis_size(axis))
    route = [(i - distance, i) for i in devices if i - distance in devices]
    return lax.ppermute(block, axis, route)


def silu_parts(hidden_gate):
    sigma = jax.nn.sigmoid(hidden_gate)
    return (hidden_gate * sigma, sigma * (1.0 + hidden_gate * (1.0 - sigma)))


def project_forward(x_rows, gate_mat, up_mat):
    hidden_gate = jnp.dot(x_rows, gate_mat, preferred_element_type=jnp.float32)
    hidden_up = jnp.dot(x_rows, up_mat, preferred_element_type=jnp.float32)
    return (hidden_gate, hidden_up)


def expert_backward(hidden_gate, hidden_up, dy_rows, gate_mat, up_mat, down_mat, basis):
    act, dact = silu_parts(hidden_gate)
    activ = (act * hidden_up).astype(jnp.bfloat16)
    grad_act = lax.dot_general(
        dy_rows, down_mat, (((1,), (1,)), ((), ())), preferred_element_type=jnp.float32
    )
    grad_gate = (grad_act * hidden_up * dact).astype(jnp.bfloat16)
    grad_up = (grad_act * act).astype(jnp.bfloat16)
    dx_rows = (
        lax.dot_general(
            grad_gate, gate_mat, (((1,), (1,)), ((), ())), preferred_element_type=jnp.float32
        )
        + lax.dot_general(
            grad_up, up_mat, (((1,), (1,)), ((), ())), preferred_element_type=jnp.float32
        )
    ).astype(jnp.bfloat16)
    rotated = jnp.dot(activ, basis, preferred_element_type=jnp.float32).astype(jnp.bfloat16)
    rot_sq = (rotated.astype(jnp.float32) ** 2).astype(jnp.bfloat16)
    dy_sq = (dy_rows.astype(jnp.float32) ** 2).astype(jnp.bfloat16)
    return (dx_rows, rotated, rot_sq, dy_sq)


def dispatch_matrix(ids, expert_count, capacity):
    flat = ids.reshape(-1)
    pairs = flat.shape[0]
    onehot = (flat[:, None] == jnp.arange(expert_count, dtype=jnp.int32)[None, :]).astype(
        jnp.float32
    )
    row_pos = lax.broadcasted_iota(jnp.int32, (pairs, pairs), 0)
    col_pos = lax.broadcasted_iota(jnp.int32, (pairs, pairs), 1)
    earlier = (row_pos > col_pos).astype(jnp.float32)
    prior = jnp.dot(
        earlier, onehot, precision=lax.Precision.HIGHEST, preferred_element_type=jnp.float32
    )
    rank = jnp.sum(prior * onehot, axis=1).astype(jnp.int32)
    slots = flat * capacity + rank
    targets = jnp.arange(expert_count * capacity, dtype=jnp.int32)
    return (targets[:, None] == slots[None, :]).astype(jnp.bfloat16)


def spread_rows(matrix, token_rows):
    return jnp.dot(matrix, token_rows, preferred_element_type=jnp.float32).astype(jnp.bfloat16)


def shards(saved_input, out_grad, expert_ids, router_weights, w_gate, w_up, w_down, eigenbasis):
    segment_count = lax.axis_size("segment")
    expert_count = lax.axis_size("expert")
    segment_here = lax.axis_index("segment")
    micro_count = saved_input.shape[1]
    tokens_dev = saved_input.shape[2]
    width = saved_input.shape[3]
    capacity = max(2, 4 * tokens_dev // expert_count)
    buffer_rows = expert_count * capacity
    gate_mat = w_gate[0, 0]
    up_mat = w_up[0, 0]
    down_mat = w_down[0, 0]
    basis = eigenbasis[0, 0]
    hidden_width = gate_mat.shape[1]
    matrices = jnp.stack(
        [
            dispatch_matrix(expert_ids[0, micro], expert_count, capacity)
            for micro in range(micro_count)
        ]
    )
    x_send = jnp.stack(
        [
            spread_rows(matrices[micro], jnp.repeat(saved_input[0, micro], 2, axis=0))
            for micro in range(micro_count)
        ]
    )
    x_recv = lax.all_to_all(
        x_send.reshape(micro_count, expert_count, capacity, width),
        "expert",
        split_axis=1,
        concat_axis=1,
        tiled=True,
    )
    gate_all, up_all = project_forward(
        x_recv.reshape(micro_count * buffer_rows, width), gate_mat, up_mat
    )
    gate_all = gate_all.reshape(micro_count, buffer_rows, hidden_width)
    up_all = up_all.reshape(micro_count, buffer_rows, hidden_width)
    rotated_list = []
    dy_list = []
    rot_sq_list = []
    dy_sq_list = []
    grads_out = jnp.zeros((micro_count, tokens_dev, width), jnp.bfloat16)
    received = jnp.zeros((tokens_dev, width), jnp.bfloat16)
    zero_rows = jnp.zeros((tokens_dev, width), jnp.bfloat16)
    total_ticks = micro_count + segment_count - 1
    for tick_index in range(total_ticks):
        micro_now = tick_index - (segment_count - 1 - segment_here)
        valid = jnp.logical_and(micro_now >= 0, micro_now < micro_count)
        index = jnp.clip(micro_now, 0, micro_count - 1)
        last_grad = lax.dynamic_index_in_dim(out_grad, index, 0, keepdims=False)
        upstream = jnp.where(segment_here == segment_count - 1, last_grad, received)
        upstream = jnp.where(valid, upstream, zero_rows)
        matrix = lax.dynamic_index_in_dim(matrices, index, 0, keepdims=False)
        weights_now = lax.dynamic_index_in_dim(router_weights[0], index, 0, keepdims=False)
        dy_tok = (
            weights_now.reshape(-1, 1) * jnp.repeat(upstream.astype(jnp.float32), 2, axis=0)
        ).astype(jnp.bfloat16)
        dy_send = spread_rows(matrix, dy_tok).reshape(expert_count, capacity, width)
        dy_rows = lax.all_to_all(
            dy_send, "expert", split_axis=0, concat_axis=0, tiled=True
        ).reshape(buffer_rows, width)
        hidden_gate = lax.dynamic_index_in_dim(gate_all, index, 0, keepdims=False)
        hidden_up = lax.dynamic_index_in_dim(up_all, index, 0, keepdims=False)
        dx_rows, rotated, rot_sq, dy_sq = expert_backward(
            hidden_gate, hidden_up, dy_rows, gate_mat, up_mat, down_mat, basis
        )
        rotated_list.append(rotated)
        dy_list.append(dy_rows)
        rot_sq_list.append(rot_sq)
        dy_sq_list.append(dy_sq)
        back = lax.all_to_all(
            dx_rows.reshape(expert_count, capacity, width),
            "expert",
            split_axis=0,
            concat_axis=0,
            tiled=True,
        ).reshape(buffer_rows, width)
        picked = lax.dot_general(
            matrix, back, (((0,), (0,)), ((), ())), preferred_element_type=jnp.float32
        ).reshape(tokens_dev, 2, width)
        grad_in = (upstream.astype(jnp.float32) + picked[:, 0] + picked[:, 1]).astype(jnp.bfloat16)
        updated = lax.dynamic_update_index_in_dim(grads_out, grad_in, index, 0)
        grads_out = jnp.where(valid, updated, grads_out)
        if tick_index + 1 < total_ticks:
            received = passed_along(grad_in, "segment", -1)
    all_rotated = jnp.concatenate(rotated_list, axis=0)
    all_dy = jnp.concatenate(dy_list, axis=0)
    all_rot_sq = jnp.concatenate(rot_sq_list, axis=0)
    all_dy_sq = jnp.concatenate(dy_sq_list, axis=0)
    grad_sum = lax.dot_general(
        all_rotated, all_dy, (((0,), (0,)), ((), ())), preferred_element_type=jnp.float32
    )
    scale_sum = lax.dot_general(
        all_rot_sq, all_dy_sq, (((0,), (0,)), ((), ())), preferred_element_type=jnp.float32
    )
    rotated_grad = (grad_sum * (1.0 / micro_count)).astype(jnp.bfloat16)
    ekfac_scales = scale_sum * (1.0 / micro_count)
    return (grads_out[None], rotated_grad[None, None], ekfac_scales[None, None])


def dot_f32(a, b, dims):
    return lax.dot_general(a, b, (dims, ((), ())), preferred_element_type=jnp.float32)


def relay_kernel(
    cap,
    x_ref,
    og_ref,
    ids_ref,
    rw_ref,
    gate_hbm,
    up_hbm,
    down_hbm,
    basis_hbm,
    gin_out,
    rot_out,
    scale_out,
    gate,
    up,
    down,
    basis,
    x_send,
    x_recv,
    dy_send,
    dy_recv,
    dx_send,
    dx_recv,
    x_peer,
    g_peer,
    part_send,
    part_recv,
    own_part,
    g_recv,
    gin,
    hid_g,
    hid_u,
    rot_t,
    rsq_t,
    spread_m,
    combine,
    slot_w,
    ids_peer,
    rw_peer,
    rot_v,
    scale_v,
    w_sem,
    send_sem,
    recv_sem,
    self_sem,
    swap_send,
    swap_recv,
    meta_send,
    meta_recv,
    relay_send,
    relay_recv,
    out_sem,
    go_sem,
):
    bf16 = jnp.bfloat16
    f32 = jnp.float32
    n = lax.axis_size("expert")
    segs = lax.axis_size("segment")
    me = lax.axis_index("expert")
    seg = lax.axis_index("segment")
    micros, tokens, width = x_ref.shape
    half = n // 2
    local = lax.rem(me, half)
    base = me - local
    partner = lax.rem(me + half, n)
    rows = half * cap
    OWN, PEER = 0, 1
    step = min(512, width)
    pieces = [slice(c * step, (c + 1) * step) for c in range(width // step)]
    is_last = seg == segs - 1
    inner = (me >= half) == (local < half // 2)
    X, DY, DX = 0, 1, 2
    GX, GG, GP = 0, 1, 2

    weights = [
        pltpu.make_async_copy(src, dst, w_sem.at[i])
        for i, (src, dst) in enumerate(
            ((gate_hbm, gate), (up_hbm, up), (down_hbm, down), (basis_hbm, basis))
        )
    ]
    for w in weights:
        w.start()

    barrier = pltpu.get_barrier_semaphore()

    def greet(d, carry):
        peer = base + lax.rem(local + d, half)
        pl.semaphore_signal(barrier, inc=1, device_id={"expert": peer})
        return carry

    lax.fori_loop(1, half, greet, 0)
    pl.semaphore_signal(barrier, inc=1, device_id={"expert": partner})

    @pl.when(seg > 0)
    def _():
        pl.semaphore_signal(barrier, inc=1, device_id={"segment": seg - 1})

    @pl.when(seg < segs - 1)
    def _():
        pl.semaphore_signal(barrier, inc=1, device_id={"segment": seg + 1})

    def block(side, i):
        return pl.ds(pl.multiple_of(side * rows + i * cap, cap), cap)

    def push(kind, side, m, src, dst):
        here = block(side, local)
        pltpu.make_async_copy(
            src.at[m, here], dst.at[m, here], self_sem.at[kind, side, m]
        ).start()

        def one(d, carry):
            other = lax.rem(local + d, half)
            pltpu.make_async_remote_copy(
                src_ref=src.at[m, block(side, other)],
                dst_ref=dst.at[m, here],
                send_sem=send_sem.at[kind, side, m],
                recv_sem=recv_sem.at[kind, side, m],
                device_id={"expert": base + other},
            ).start()
            return carry

        lax.fori_loop(1, half, one, 0)

    def whole(kind, side, m, src, dst):
        part = pl.ds(side * rows, (half - 1) * cap)
        return pltpu.make_async_remote_copy(
            src_ref=src.at[m, part],
            dst_ref=dst.at[m, part],
            send_sem=send_sem.at[kind, side, m],
            recv_sem=recv_sem.at[kind, side, m],
            device_id={"expert": base + lax.rem(local + 1, half)},
        )

    def arrive(kind, side, m, src, dst):
        here = block(side, local)
        pltpu.make_async_copy(
            src.at[m, here], dst.at[m, here], self_sem.at[kind, side, m]
        ).wait()
        whole(kind, side, m, src, dst).wait_recv()

    def swap(kind, m, src, dst):
        return pltpu.make_async_remote_copy(
            src_ref=src.at[m],
            dst_ref=dst.at[m],
            send_sem=swap_send.at[kind, m],
            recv_sem=swap_recv.at[kind, m],
            device_id={"expert": partner},
        )

    metas = [
        pltpu.make_async_remote_copy(
            src_ref=src,
            dst_ref=dst,
            send_sem=meta_send.at[i],
            recv_sem=meta_recv.at[i],
            device_id={"expert": partner},
        )
        for i, (src, dst) in enumerate(((ids_ref, ids_peer), (rw_ref, rw_peer)))
    ]

    def matrices(side, ids, rw):
        row_t = lax.broadcasted_iota(jnp.int32, (tokens, tokens), 0)
        col_t = lax.broadcasted_iota(jnp.int32, (tokens, tokens), 1)
        earlier = (row_t < col_t).astype(bf16)
        experts = lax.broadcasted_iota(jnp.int32, (n, tokens), 0)
        slots = lax.broadcasted_iota(jnp.int32, (rows, tokens), 0)
        for m in range(micros):
            ids0 = ids[m, 0:1, :]
            ids1 = ids[m, 1:2, :]
            hot0 = (experts == ids0).astype(f32)
            hot1 = (experts == ids1).astype(f32)
            prior = dot_f32((hot0 + hot1).astype(bf16), earlier, ((1,), (0,)))
            rank0 = jnp.sum(prior * hot0, axis=0, keepdims=True).astype(jnp.int32)
            rank1 = jnp.sum(prior * hot1, axis=0, keepdims=True).astype(jnp.int32)
            pick0 = (slots == (ids0 - base) * cap + rank0).astype(f32)
            pick1 = (slots == (ids1 - base) * cap + rank1).astype(f32)
            both = pick0 + pick1
            weighted = pick0 * rw[m, 0:1, :] + pick1 * rw[m, 1:2, :]
            spread_m[m, side] = both.astype(bf16)
            combine[m, side] = jnp.transpose(both).astype(bf16)
            slot_w[m, side] = jnp.sum(weighted, axis=1, keepdims=True)

    def send_x(side, m, src):
        for cols in pieces:
            moved = dot_f32(spread_m[m, side], src[m, :, cols], ((1,), (0,)))
            x_send[m, side * rows : (side + 1) * rows, cols] = moved.astype(bf16)
        push(X, side, m, x_send, x_recv)

    def send_dy(side, m, src):
        for cols in pieces:
            moved = dot_f32(spread_m[m, side], src[m, :, cols], ((1,), (0,)))
            dy_send[m, side * rows : (side + 1) * rows, cols] = (
                slot_w[m, side] * moved
            ).astype(bf16)
        push(DY, side, m, dy_send, dy_recv)

    def begin_x(m):
        pl.when(inner)(swap(GX, m, x_ref, x_peer).start)
        send_x(OWN, m, x_ref)
        pl.when(jnp.logical_not(inner))(swap(GX, m, x_ref, x_peer).start)

    def begin_dy(m, g_ref):
        pl.when(inner)(swap(GG, m, g_ref, g_peer).start)
        send_dy(OWN, m, g_ref)
        pl.when(jnp.logical_not(inner))(swap(GG, m, g_ref, g_peer).start)

    def peer_x(m):
        swap(GX, m, x_ref, x_peer).wait_recv()
        send_x(PEER, m, x_peer)

    def peer_dy(m, g_ref):
        swap(GG, m, g_ref, g_peer).wait_recv()
        send_dy(PEER, m, g_peer)

    def forward(m):
        arrive(X, OWN, m, x_send, x_recv)
        arrive(X, PEER, m, x_send, x_recv)
        x = x_recv[m]
        hid_g[m] = dot_f32(x, gate[...], ((1,), (0,)))
        hid_u[m] = dot_f32(x, up[...], ((1,), (0,)))

    def backward(m):
        arrive(DY, OWN, m, dy_send, dy_recv)
        arrive(DY, PEER, m, dy_send, dy_recv)
        grad_act = dot_f32(dy_recv[m], down[...], ((1,), (1,)))
        hg = hid_g[m]
        hu = hid_u[m]
        act, dact = silu_parts(hg)
        grad_gate = (grad_act * hu * dact).astype(bf16)
        grad_up = (grad_act * act).astype(bf16)
        for cols in pieces:
            dx_send[m, :, cols] = (
                dot_f32(grad_gate, gate[cols, :], ((1,), (1,)))
                + dot_f32(grad_up, up[cols, :], ((1,), (1,)))
            ).astype(bf16)
        push(DX, PEER, m, dx_send, dx_recv)
        push(DX, OWN, m, dx_send, dx_recv)

    def rotate(m):
        act, _ = silu_parts(hid_g[m])
        activ = (act * hid_u[m]).astype(bf16)
        rotated = dot_f32(activ, basis[...], ((1,), (0,))).astype(bf16).astype(f32)
        turned = jnp.transpose(rotated)
        rot_t[m] = turned.astype(bf16)
        rsq_t[m] = (turned * turned).astype(bf16)

    def relay(m):
        return pltpu.make_async_remote_copy(
            src_ref=gin.at[m],
            dst_ref=g_recv.at[m],
            send_sem=relay_send.at[m],
            recv_sem=relay_recv.at[m],
            device_id={"segment": lax.rem(seg + segs - 1, segs)},
        )

    def half_back(m):
        arrive(DX, PEER, m, dx_send, dx_recv)
        for cols in pieces:
            theirs = dot_f32(combine[m, PEER], dx_recv[m, rows:, cols], ((1,), (0,)))
            part_send[m, :, cols] = theirs.astype(bf16)
        swap(GP, m, part_send, part_recv).start()

    def own_back(m, g_ref):
        arrive(DX, OWN, m, dx_send, dx_recv)
        for cols in pieces:
            mine = dot_f32(combine[m, OWN], dx_recv[m, :rows, cols], ((1,), (0,)))
            own_part[m, :, cols] = g_ref[m, :, cols].astype(f32) + mine

    def finish(m):
        swap(GP, m, part_send, part_recv).wait_recv()
        gin[m] = (own_part[m] + part_recv[m].astype(f32)).astype(bf16)

        @pl.when(seg > 0)
        def _():
            relay(m).start()

        pltpu.make_async_copy(gin.at[m], gin_out.at[m], out_sem.at[2 + m]).start()

    def statistics():
        part = min(256, width)

        def one(c, carry):
            cols = pl.ds(pl.multiple_of(c * part, part), part)
            grad = jnp.zeros((rot_v.shape[0], part), f32)
            scale = jnp.zeros((rot_v.shape[0], part), f32)
            for m in range(micros):
                dy = dy_recv[m, :, cols]
                wide = dy.astype(f32)
                grad = grad + dot_f32(rot_t[m], dy, ((1,), (0,)))
                scale = scale + dot_f32(rsq_t[m], (wide * wide).astype(bf16), ((1,), (0,)))
            rot_v[:, cols] = (grad * (1.0 / micros)).astype(bf16)
            scale_v[:, cols] = scale * (1.0 / micros)
            return carry

        lax.fori_loop(0, width // part, one, 0)
        pltpu.make_async_copy(rot_v, rot_out, out_sem.at[0]).start()
        pltpu.make_async_copy(scale_v, scale_out, out_sem.at[1]).start()

    def per_micro(fn):
        def one(m, carry):
            fn(m)
            return carry

        lax.fori_loop(0, micros, one, 0)

    matrices(OWN, ids_ref, rw_ref)
    neighbours = jnp.minimum(seg, 1) + jnp.minimum(segs - 1 - seg, 1)
    pl.semaphore_wait(barrier, half + neighbours)
    for meta in metas:
        meta.start()

    @pl.when(is_last)
    def _():
        begin_dy(0, og_ref)
        begin_x(0)
        for meta in metas:
            meta.wait_recv()
        matrices(PEER, ids_peer, rw_peer)
        for w in weights:
            w.wait()

        def through(m, carry):
            peer_dy(m - 1, og_ref)
            begin_dy(m, og_ref)
            peer_x(m - 1)
            begin_x(m)
            forward(m - 1)
            backward(m - 1)
            return carry

        lax.fori_loop(1, micros, through, 0)
        peer_dy(micros - 1, og_ref)
        if segs > 1:
            pl.semaphore_signal(go_sem, inc=1, device_id={"segment": seg - 1})
        peer_x(micros - 1)
        forward(micros - 1)
        backward(micros - 1)

        def back(m):
            half_back(m)
            own_back(m, og_ref)
            finish(m)

        per_micro(back)
        per_micro(rotate)
        statistics()

    @pl.when(jnp.logical_not(is_last))
    def _():
        for meta in metas:
            meta.wait_recv()
        matrices(PEER, ids_peer, rw_peer)

        @pl.when(seg == segs - 2)
        def _():
            pl.semaphore_wait(go_sem, 1)

        begin_x(0)
        peer_x(0)
        for w in weights:
            w.wait()
        forward(0)
        rotate(0)

        def begin(m):
            relay(m).wait_recv()
            begin_dy(m, g_recv)

        begin(0)

        def through(m, carry):
            begin_x(m)
            peer_dy(m - 1, g_recv)
            peer_x(m)
            begin(m)
            backward(m - 1)
            forward(m)
            rotate(m)
            return carry

        lax.fori_loop(1, micros, through, 0)
        peer_dy(micros - 1, g_recv)
        backward(micros - 1)
        half_back(0)
        statistics()
        own_back(0, g_recv)
        finish(0)

        def back(m, carry):
            half_back(m)
            own_back(m, g_recv)
            finish(m)
            return carry

        lax.fori_loop(1, micros, back, 0)

    for meta in metas:
        meta.wait_send()

    def drain(m):
        for side in (OWN, PEER):
            whole(X, side, m, x_send, x_recv).wait_send()
            whole(DY, side, m, dy_send, dy_recv).wait_send()
            whole(DX, side, m, dx_send, dx_recv).wait_send()
        swap(GX, m, x_ref, x_peer).wait_send()
        swap(GG, m, g_recv, g_peer).wait_send()
        swap(GP, m, part_send, part_recv).wait_send()

        @pl.when(seg > 0)
        def _():
            relay(m).wait_send()

        pltpu.make_async_copy(gin.at[m], gin_out.at[m], out_sem.at[2 + m]).wait()

    per_micro(drain)
    pltpu.make_async_copy(rot_v, rot_out, out_sem.at[0]).wait()
    pltpu.make_async_copy(scale_v, scale_out, out_sem.at[1]).wait()


def fused_shards(
    saved_input, out_grad, expert_ids, router_weights, w_gate, w_up, w_down, eigenbasis
):
    n = lax.axis_size("expert")
    micros, tokens, width = saved_input.shape[1:]
    cap = max(2, 4 * tokens // n)
    if cap % 16 or n % 2:
        return shards(
            saved_input, out_grad, expert_ids, router_weights, w_gate, w_up, w_down, eigenbasis
        )
    rows = n * cap
    hidden = w_gate.shape[3]
    bf16 = jnp.bfloat16
    f32 = jnp.float32
    vmem = pl.BlockSpec(memory_space=pltpu.VMEM)
    anywhere = pl.BlockSpec(memory_space=pl.ANY)
    in_hbm = pl.BlockSpec(memory_space=pltpu.MemorySpace.HBM)
    routed = pltpu.VMEM((micros, rows, width), bf16)
    block = pltpu.VMEM((micros, tokens, width), bf16)
    grad_in, rotated_grad, scales = pl.pallas_call(
        functools.partial(relay_kernel, cap),
        name="relay",
        out_shape=(
            jax.ShapeDtypeStruct((micros, tokens, width), bf16),
            jax.ShapeDtypeStruct((hidden, width), bf16),
            jax.ShapeDtypeStruct((hidden, width), f32),
        ),
        in_specs=[vmem] * 4 + [in_hbm] * 4,
        out_specs=(anywhere, anywhere, anywhere),
        scratch_shapes=[
            pltpu.VMEM((width, hidden), bf16),
            pltpu.VMEM((width, hidden), bf16),
            pltpu.VMEM((hidden, width), bf16),
            pltpu.VMEM((hidden, hidden), bf16),
            routed,
            routed,
            routed,
            routed,
            routed,
            routed,
            block,
            block,
            block,
            block,
            pltpu.VMEM((micros, tokens, width), f32),
            block,
            block,
            pltpu.VMEM((micros, rows, hidden), f32),
            pltpu.VMEM((micros, rows, hidden), f32),
            pltpu.VMEM((micros, hidden, rows), bf16),
            pltpu.VMEM((micros, hidden, rows), bf16),
            pltpu.VMEM((micros, 2, rows // 2, tokens), bf16),
            pltpu.VMEM((micros, 2, tokens, rows // 2), bf16),
            pltpu.VMEM((micros, 2, rows // 2, 1), f32),
            pltpu.VMEM((micros, 2, tokens), jnp.int32),
            pltpu.VMEM((micros, 2, tokens), f32),
            pltpu.VMEM((hidden, width), bf16),
            pltpu.VMEM((hidden, width), f32),
            pltpu.SemaphoreType.DMA((4,)),
            pltpu.SemaphoreType.DMA((3, 2, micros)),
            pltpu.SemaphoreType.DMA((3, 2, micros)),
            pltpu.SemaphoreType.DMA((3, 2, micros)),
            pltpu.SemaphoreType.DMA((3, micros)),
            pltpu.SemaphoreType.DMA((3, micros)),
            pltpu.SemaphoreType.DMA((2,)),
            pltpu.SemaphoreType.DMA((2,)),
            pltpu.SemaphoreType.DMA((micros,)),
            pltpu.SemaphoreType.DMA((micros,)),
            pltpu.SemaphoreType.DMA((2 + micros,)),
            pltpu.SemaphoreType.REGULAR,
        ],
        compiler_params=pltpu.CompilerParams(
            collective_id=0, has_side_effects=True, vmem_limit_bytes=62 << 20
        ),
    )(
        saved_input[0],
        out_grad,
        jnp.swapaxes(expert_ids[0], 1, 2),
        jnp.swapaxes(router_weights[0], 1, 2),
        w_gate[0, 0],
        w_up[0, 0],
        w_down[0, 0],
        eigenbasis[0, 0],
    )
    return (grad_in[None], rotated_grad[None, None], scales[None, None])


def solution(mesh):
    in_specs = (
        P("segment", None, "expert", None),
        P(None, "expert", None),
        P("segment", None, "expert", None),
        P("segment", None, "expert", None),
        P("segment", "expert", None, None),
        P("segment", "expert", None, None),
        P("segment", "expert", None, None),
        P("segment", "expert", None, None),
    )
    out_specs = (
        P("segment", None, "expert", None),
        P("segment", "expert", None, None),
        P("segment", "expert", None, None),
    )
    return jax.shard_map(
        fused_shards, mesh=mesh, in_specs=in_specs, out_specs=out_specs, check_vma=False)
```
